512 devices in a mesh: row: 16 (over y, core), col: 32 (over x, z).
Axes of the slice: x: 4, y: 8, z: 8, core: 2. Of those that a mesh axis runs over, the one named last changes fastest.
Arguments:
- features: float32 [16384, 1536], P('row', 'col'), may hold values from -6 to 6
Outputs:
- panel: float32 [16384, 512], P('row')
- trailing: float32 [16384, 16384], P('row', 'col')
The draws below stay inside these ranges and needn't reach their ends.
All inputs are finite; a program needn't handle non-finite values.
Results may differ from the reference program's by a relative error of at most 0.0003.
Values sent between devices are 32-bit elements; how exact they have to be, the bound alone decides.
No kernel may reach another device: no remote copies, remote signals or barrier semaphores. Data moves between devices by JAX's collectives and lax.ppermute only.
A program may use at most 64 MiB of HBM per device.

```python
import jax
import jax.numpy as jnp
from jax import lax

D = 1536
PANEL = 512
ORDER = 16384


def level_of(own_key, extent, cuts, smallest, high):
    gain = 1.0
    for axis_at, parts in cuts:
        draws = jax.random.uniform(jax.random.fold_in(jax.random.fold_in(own_key, 6), axis_at), (parts,), jnp.float32, smallest / len(cuts), high / len(cuts))
        gain = gain * jnp.repeat(jnp.exp(draws), extent[axis_at] // parts).reshape((-1,) + (1,) * (len(extent) - 1 - axis_at))
    return gain


def bell_draw(key, extent, width, reach, split=(), held_as=jnp.bfloat16):
    result = width * jax.random.normal(key, extent, jnp.float32)
    if split:
        result = result * level_of(key, extent, split, -0.22, 0.18)
    return jnp.clip(result, -reach, reach).astype(held_as)


def setup_inputs(seed: int = 0) -> dict:
    key_of = jax.random.split(jax.random.key(seed), 2)
    return {
        "features": bell_draw(key_of[0], (ORDER, D), 1.0, 6.0, ((0, 16), (1, 32)), jnp.float32),
    }


gamma_scale = 0.6
ridge_value = 0.05

def gauss_tile(left_rows, right_rows, row_start, col_start):
    left_sq = jnp.sum(left_rows * left_rows, axis=1)
    right_sq = jnp.sum(right_rows * right_rows, axis=1)
    inner_prod = jnp.dot(left_rows.astype(jnp.float32), right_rows.T.astype(jnp.float32), precision=lax.Precision.HIGHEST, preferred_element_type=jnp.float32)
    distance = left_sq[:, None] + right_sq[None, :] - 2.0 * inner_prod
    kernel_value = jnp.exp(-distance * (gamma_scale / D))
    row_index = row_start + jnp.arange(left_rows.shape[0], dtype=jnp.int32)
    col_index = col_start + jnp.arange(right_rows.shape[0], dtype=jnp.int32)
    return kernel_value + jnp.where(row_index[:, None] == col_index[None, :], ridge_value, 0.0).astype(jnp.float32)

def reference(features):
    blocks = features.shape[0] // PANEL
    head_rows = features[:PANEL]
    corner = gauss_tile(head_rows, head_rows, 0, 0)
    chol_factor = jnp.linalg.cholesky(corner)
    inverse = lax.linalg.triangular_solve(chol_factor, jnp.eye(PANEL, dtype=jnp.float32), left_side=True, lower=True)
    starts = (jnp.arange(blocks, dtype=jnp.int32) * PANEL).astype(jnp.int32)

    def panel_block(block_start):
        block_rows = lax.dynamic_slice_in_dim(features, block_start, PANEL, 0)
        side_tile = gauss_tile(block_rows, head_rows, block_start, 0)
        return jnp.dot(side_tile.astype(jnp.float32), inverse.T.astype(jnp.float32), precision=lax.Precision.HIGHEST, preferred_element_type=jnp.float32)
    solved = lax.map(panel_block, starts).reshape(features.shape[0], PANEL)
    panel_out = jnp.concatenate([chol_factor, solved[PANEL:]], axis=0)
    masked = jnp.concatenate([jnp.zeros((PANEL, PANEL), jnp.float32), solved[PANEL:]], axis=0)

    def trailing_block(block_start):
        block_rows = lax.dynamic_slice_in_dim(features, block_start, PANEL, 0)
        kernel_tile = gauss_tile(block_rows, features, block_start, 0)
        block_panel = lax.dynamic_slice_in_dim(masked, block_start, PANEL, 0)
        return kernel_tile - jnp.dot(block_panel.astype(jnp.float32), masked.T.astype(jnp.float32), precision=lax.Precision.HIGHEST, preferred_element_type=jnp.float32)
    trailing = lax.map(trailing_block, starts).reshape(features.shape[0], features.shape[0])
    return (panel_out, trailing)
```

```python
import jax
import jax.numpy as jnp
from jax import lax
from jax.experimental import pallas as pl
from jax.experimental.pallas import tpu as pltpu
from jax.sharding import Mesh
from jax.sharding import PartitionSpec as P

D = 1536
PANEL = 512
BLOCK = 128
GROUP = 4
TALL = 256
ROW = ("y", "core")
COL = ("x", "z")
YS, CORES, XS, ZS = 8, 2, 4, 8


gamma_scale = 0.6
ridge_value = 0.05


def full(a, b):
    return jnp.dot(a, b, precision=lax.Precision.HIGHEST, preferred_element_type=jnp.float32)


def product(a, b, on_a, on_b, precision=lax.Precision.HIGHEST):
    return lax.dot_general(
        a, b, (((on_a,), (on_b,)), ((), ())), precision=precision, preferred_element_type=jnp.float32
    )


def factor_block(rows):
    sub = lax.broadcasted_iota(jnp.int32, (8, BLOCK), 0)
    lane = lax.broadcasted_iota(jnp.int32, (8, BLOCK), 1)
    count = BLOCK // 8
    rows = list(rows)
    unit = [jnp.where(lane == sub + 8 * v, 1.0, 0.0).astype(jnp.float32) for v in range(count)]
    scale = [jnp.zeros((8, BLOCK), jnp.float32) for _ in range(count)]

    def column(v, j):
        return jnp.broadcast_to(rows[v][:, j : j + 1], (8, BLOCK))

    for start in range(0, BLOCK, GROUP):
        v0, o = start // 8, start % 8
        head = [column(v0, start + k) for k in range(GROUP)]
        inv, coef = [], {}
        for k in range(GROUP):
            pivot = head[k][o + k : o + k + 1, :]
            inv.append(1.0 / pivot)
            root = lax.rsqrt(pivot)
            scale[v0] = jnp.where(sub == o + k, root, scale[v0])
            for l in range(k + 1, GROUP):
                coef[k, l] = inv[k] * head[k][o + l : o + l + 1, :]
                head[l] = head[l] - head[k] * coef[k, l]
        top = [rows[v0][o + k : o + k + 1, :] for k in range(GROUP)]
        top_unit = [unit[v0][o + k : o + k + 1, :] for k in range(GROUP)]
        for k in range(GROUP):
            for l in range(k + 1, GROUP):
                top[l] = top[l] - coef[k, l] * top[k]
                top_unit[l] = top_unit[l] - coef[k, l] * top_unit[k]
        for v in range(v0, count):
            if v == v0:
                part = head
            else:
                part = [column(v, start + k) for k in range(GROUP)]
                for k in range(GROUP):
                    for l in range(k + 1, GROUP):
                        part[l] = part[l] - part[k] * coef[k, l]
            new_row, new_unit = rows[v], unit[v]
            for k in range(GROUP):
                factor = part[k] * inv[k]
                if v == v0:
                    factor = jnp.where(sub > o + k, factor, 0.0)
                new_row = new_row - factor * top[k]
                new_unit = new_unit - factor * top_unit[k]
            rows[v], unit[v] = new_row, new_unit
    rows = [jnp.where(lane >= sub + 8 * v, rows[v] * scale[v], 0.0) for v in range(count)]
    unit = [unit[v] * scale[v] for v in range(count)]
    return jnp.concatenate(rows, axis=0), jnp.concatenate(unit, axis=0)


def factor_kernel(corner_ref, lower_ref, inverse_ref, work_ref):
    work_ref[...] = corner_ref[...]
    inverse_ref[...] = jnp.zeros((PANEL, PANEL), jnp.float32)

    def update(at, upper, inv):
        end = at + BLOCK
        lower_ref[at:end, at:end] = upper.T
        if at:
            inverse_ref[at:end, :at] = full(inv, inverse_ref[at:end, :at])
        inverse_ref[at:end, at:end] = inv
        if end < PANEL:
            lower_ref[at:end, end:] = jnp.zeros((BLOCK, PANEL - end), jnp.float32)
            right = full(inv, work_ref[at:end, end:])
            below = right.T
            lower_ref[end:, at:end] = below
            work_ref[end:, end:] -= full(below, right)
            inverse_ref[end:, :end] -= full(below, inverse_ref[at:end, :end])

    @pl.loop(0, PANEL // BLOCK)
    def _(index):
        at = pl.multiple_of(index * BLOCK, BLOCK)
        block = work_ref[pl.ds(at, BLOCK), pl.ds(at, BLOCK)]
        upper, inv = factor_block([block[8 * v : 8 * v + 8] for v in range(BLOCK // 8)])
        for which in range(PANEL // BLOCK):

            @pl.when(index == which)
            def _():
                update(which * BLOCK, upper, inv)


def factor(corner):
    square = jax.ShapeDtypeStruct((PANEL, PANEL), jnp.float32)
    return pl.pallas_call(
        factor_kernel, out_shape=(square, square),
        scratch_shapes=[pltpu.VMEM((PANEL, PANEL), jnp.float32)], name="factor",
    )(corner)


def tile_kernel(start_ref, row_ref, col_ref, row_sq_ref, col_sq_ref, panel_ref, far_ref, out_ref, high_ref, low_ref):
    step = pl.program_id(0)

    def split(value):
        high = value.astype(jnp.bfloat16)
        return high, (value - high.astype(jnp.float32)).astype(jnp.bfloat16)

    @pl.when(step == 0)
    def _():
        high_ref[...], low_ref[...] = split(col_ref[...])

    def inner(a, b):
        return lax.dot_general(a, b, (((0,), (0,)), ((), ())), preferred_element_type=jnp.float32)

    high, low = split(row_ref[...])
    gram = inner(high, high_ref[...]) + (inner(high, low_ref[...]) + inner(low, high_ref[...]))
    distance = row_sq_ref[...] + col_sq_ref[...] - 2.0 * gram
    tile = jnp.exp(-distance * (gamma_scale / D))
    row = lax.broadcasted_iota(jnp.int32, tile.shape, 0) + (start_ref[0] + step * tile.shape[0])
    col = lax.broadcasted_iota(jnp.int32, tile.shape, 1) + start_ref[1]
    tile = tile + jnp.where(row == col, ridge_value, 0.0)
    out_ref[...] = tile - full(panel_ref[...], far_ref[...])


def trailing_tile(starts, row_feat, col_feat, row_sq, col_sq, panel, far):
    depth, height = row_feat.shape
    width = col_feat.shape[1]
    return pl.pallas_call(
        tile_kernel,
        out_shape=jax.ShapeDtypeStruct((height, width), jnp.float32),
        grid_spec=pltpu.PrefetchScalarGridSpec(
            num_scalar_prefetch=1,
            grid=(height // TALL,),
            in_specs=[
                pl.BlockSpec((depth, TALL), lambda i, s: (0, i)),
                pl.BlockSpec((depth, width), lambda i, s: (0, 0)),
                pl.BlockSpec((TALL, 1), lambda i, s: (i, 0)),
                pl.BlockSpec((1, width), lambda i, s: (0, 0)),
                pl.BlockSpec((TALL, PANEL), lambda i, s: (i, 0)),
                pl.BlockSpec((PANEL, width), lambda i, s: (0, 0)),
            ],
            out_specs=pl.BlockSpec((TALL, width), lambda i, s: (i, 0)),
            scratch_shapes=[pltpu.VMEM((depth, width), jnp.bfloat16)] * 2,
        ),
        name="trailing_tile",
    )(starts, row_feat, col_feat, row_sq[:, None], col_sq[None, :], panel, far)


def gauss(left, right, left_sq, right_sq):
    distance = left_sq[:, None] + right_sq[None, :] - 2.0 * product(left, right, 0, 0, lax.Precision.HIGH)
    return jnp.exp(-distance * (gamma_scale / D))


def squares(value):
    return jnp.sum(value * value, axis=0)


def ring(value, axis, size):
    at = lax.axis_index(axis)
    up = [(i, (i + 1) % size) for i in range(size)]
    down = [(target, source) for source, target in up]
    got = [(at, value)]
    above = below = value
    for step in range(1, size // 2 + 1):
        below = lax.ppermute(below, axis, up)
        got.append(((at - step) & (size - 1), below))
        if 2 * step < size:
            above = lax.ppermute(above, axis, down)
            got.append(((at + step) & (size - 1), above))
    return got


def swap(value):
    return lax.ppermute(value, "core", [(0, 1), (1, 0)])


def head_share(slices):
    y, core = lax.axis_index("y"), lax.axis_index("core")
    half = PANEL // CORES
    other = lax.ppermute(slices[:, half:PANEL], "core", [(0, 1)])
    own = jnp.where(core == 0, slices[:, :half], other)
    span = YS // 2
    while span:
        moved = lax.ppermute(own, "y", [(i, i + span) for i in range(0, YS, 2 * span)])
        own = jnp.where(y & (2 * span - 1) == span, moved, own)
        span //= 2
    return own


def head_of(own):
    core = lax.axis_index("core")
    depth, half = own.shape
    line = lax.all_gather(own, "x")
    plane = jnp.zeros((XS, ZS, depth, half), jnp.float32)
    for member, piece in ring(line, "z", ZS):
        plane = lax.dynamic_update_slice(plane, piece[:, None], (0, member, 0, 0))
    mine = plane.reshape(XS * ZS * depth, half)
    theirs = swap(mine)
    first = jnp.where(core == 0, mine, theirs)
    second = jnp.where(core == 0, theirs, mine)
    return jnp.concatenate([first, second], axis=1)


def column_share(slices):
    x, z = lax.axis_index("x"), lax.axis_index("z")
    rows, cols = YS * CORES, XS * ZS
    col = x * ZS + z
    odd = col & 1
    same, cross = [], []
    for r in range(rows):
        for c in range(cols):
            target = (c // 2 + r) % rows
            same.append((r * cols + c, target * cols + 2 * r + c % 2))
            cross.append((r * cols + c, target * cols + 2 * r + 1 - c % 2))
    left, right = slices[:, :PANEL], slices[:, PANEL:]
    like = lax.ppermute(jnp.where(odd == 0, left, right), ROW + COL, same)
    unlike = lax.ppermute(jnp.where(odd == 0, right, left), ROW + COL, cross)
    return jnp.concatenate([jnp.where(odd == 0, like, unlike), jnp.where(odd == 0, unlike, like)], axis=0)


def columns_of(piece):
    turn = (lax.axis_index("x") * ZS + lax.axis_index("z")) >> 1
    shares = lax.all_gather(piece, ROW)
    shares = lax.dynamic_slice_in_dim(jnp.concatenate([shares, shares], axis=0), turn, YS * CORES, 0)
    return shares.reshape(-1, PANEL)


def on_device(features):
    slices = features.T
    height = features.shape[0]
    row_id = lax.axis_index("y") * CORES + lax.axis_index("core")
    col_id = lax.axis_index("x") * ZS + lax.axis_index("z")
    row_feat = lax.all_gather(slices, COL, axis=0, tiled=True)
    head = head_of(head_share(slices))
    col_feat = columns_of(column_share(slices))
    head_sq = squares(head)
    eye = jnp.eye(PANEL, dtype=jnp.float32)
    corner = gauss(head, head, head_sq, head_sq) + ridge_value * eye
    lower, inverse = factor(corner)
    row_sq, col_sq = squares(row_feat), squares(col_feat)
    positions = row_id * height + jnp.arange(height, dtype=jnp.int32)
    below = positions[:, None] >= PANEL
    side = gauss(row_feat, head, row_sq, head_sq)
    solved = product(side, inverse, 1, 1)
    top = jnp.concatenate([lower, jnp.zeros((height - PANEL, PANEL), jnp.float32)], axis=0)
    panel = jnp.where(below, solved, top)
    masked = jnp.where(below, solved, 0.0)
    far = gauss(head, col_feat, head_sq, col_sq)
    far_panel = jnp.where(col_id == 0, 0.0, product(inverse, far, 1, 0))
    starts = jnp.stack([row_id * height, col_id * PANEL]).astype(jnp.int32)
    trailing = trailing_tile(starts, row_feat, col_feat, row_sq, col_sq, masked, far_panel)
    return (panel, trailing)


def solution(mesh):
    fine = Mesh(mesh.devices.reshape(YS, CORES, XS, ZS), ROW + COL)
    return jax.shard_map(
        on_device,
        mesh=fine,
        in_specs=(P(ROW, COL),),
        out_specs=(P(ROW, None), P(ROW, COL)),
        check_vma=False,
    )
```

```python
import jax
import jax.numpy as jnp
from jax import lax
from jax.experimental import pallas as pl
from jax.experimental.pallas import tpu as pltpu
from jax.sharding import Mesh
from jax.sharding import PartitionSpec as P

D = 1536
PANEL = 512
BLOCK = 128
GROUP = 4
TALL = 256
ROW = ("y", "core")
COL = ("x", "z")
YS, CORES, XS, ZS = 8, 2, 4, 8


gamma_scale = 0.6
ridge_value = 0.05


def full(a, b):
    return jnp.dot(a, b, precision=lax.Precision.HIGHEST, preferred_element_type=jnp.float32)


def product(a, b, on_a, on_b, precision=lax.Precision.HIGHEST):
    return lax.dot_general(
        a, b, (((on_a,), (on_b,)), ((), ())), precision=precision, preferred_element_type=jnp.float32
    )


def factor_block(rows):
    sub = lax.broadcasted_iota(jnp.int32, (8, BLOCK), 0)
    lane = lax.broadcasted_iota(jnp.int32, (8, BLOCK), 1)
    count = BLOCK // 8
    rows = list(rows)
    unit = [jnp.where(lane == sub + 8 * v, 1.0, 0.0).astype(jnp.float32) for v in range(count)]
    scale = [jnp.zeros((8, BLOCK), jnp.float32) for _ in range(count)]

    def column(v, j):
        return jnp.broadcast_to(rows[v][:, j : j + 1], (8, BLOCK))

    for start in range(0, BLOCK, GROUP):
        v0, o = start // 8, start % 8
        head = [column(v0, start + k) for k in range(GROUP)]
        inv, coef = [], {}
        for k in range(GROUP):
            pivot = head[k][o + k : o + k + 1, :]
            inv.append(1.0 / pivot)
            root = lax.rsqrt(pivot)
            scale[v0] = jnp.where(sub == o + k, root, scale[v0])
            for l in range(k + 1, GROUP):
                coef[k, l] = inv[k] * head[k][o + l : o + l + 1, :]
                head[l] = head[l] - head[k] * coef[k, l]
        top = [rows[v0][o + k : o + k + 1, :] for k in range(GROUP)]
        top_unit = [unit[v0][o + k : o + k + 1, :] for k in range(GROUP)]
        for k in range(GROUP):
            for l in range(k + 1, GROUP):
                top[l] = top[l] - coef[k, l] * top[k]
                top_unit[l] = top_unit[l] - coef[k, l] * top_unit[k]
        for v in range(v0, count):
            if v == v0:
                part = head
            else:
                part = [column(v, start + k) for k in range(GROUP)]
                for k in range(GROUP):
                    for l in range(k + 1, GROUP):
                        part[l] = part[l] - part[k] * coef[k, l]
            new_row, new_unit = rows[v], unit[v]
            for k in range(GROUP):
                factor = part[k] * inv[k]
                if v == v0:
                    factor = jnp.where(sub > o + k, factor, 0.0)
                new_row = new_row - factor * top[k]
                new_unit = new_unit - factor * top_unit[k]
            rows[v], unit[v] = new_row, new_unit
    rows = [jnp.where(lane >= sub + 8 * v, rows[v] * scale[v], 0.0) for v in range(count)]
    unit = [unit[v] * scale[v] for v in range(count)]
    return jnp.concatenate(rows, axis=0), jnp.concatenate(unit, axis=0)


def factor_kernel(corner_ref, lower_ref, inverse_ref, work_ref):
    work_ref[...] = corner_ref[...]
    inverse_ref[...] = jnp.zeros((PANEL, PANEL), jnp.float32)

    def update(at, upper, inv):
        end = at + BLOCK
        lower_ref[at:end, at:end] = upper.T
        if at:
            inverse_ref[at:end, :at] = full(inv, inverse_ref[at:end, :at])
        inverse_ref[at:end, at:end] = inv
        if end < PANEL:
            lower_ref[at:end, end:] = jnp.zeros((BLOCK, PANEL - end), jnp.float32)
            right = full(inv, work_ref[at:end, end:])
            below = right.T
            lower_ref[end:, at:end] = below
            work_ref[end:, end:] -= full(below, right)
            inverse_ref[end:, :end] -= full(below, inverse_ref[at:end, :end])

    @pl.loop(0, PANEL // BLOCK)
    def _(index):
        at = pl.multiple_of(index * BLOCK, BLOCK)
        block = work_ref[pl.ds(at, BLOCK), pl.ds(at, BLOCK)]
        upper, inv = factor_block([block[8 * v : 8 * v + 8] for v in range(BLOCK // 8)])
        for which in range(PANEL // BLOCK):

            @pl.when(index == which)
            def _():
                update(which * BLOCK, upper, inv)


def factor(corner):
    square = jax.ShapeDtypeStruct((PANEL, PANEL), jnp.float32)
    return pl.pallas_call(
        factor_kernel, out_shape=(square, square),
        scratch_shapes=[pltpu.VMEM((PANEL, PANEL), jnp.float32)], name="factor",
    )(corner)


def gram_of(row_high, row_low, high, low):
    def inner(a, b):
        return jnp.dot(a, b, preferred_element_type=jnp.float32)

    return inner(row_high, high) + (inner(row_high, low) + inner(row_low, high))


def split_into(value, high_ref, low_ref):
    high = value.astype(jnp.bfloat16)
    high_ref[...] = high
    low_ref[...] = (value - high.astype(jnp.float32)).astype(jnp.bfloat16)


def panel_kernel(
    start_ref, row_high_ref, row_low_ref, head_ref, row_sq_ref, head_sq_ref, inverse_ref, lower_ref,
    panel_ref, weight_ref, high_ref, low_ref,
):
    step = pl.program_id(0)

    @pl.when(step == 0)
    def _():
        split_into(head_ref[...], high_ref, low_ref)

    gram = gram_of(row_high_ref[...], row_low_ref[...], high_ref[...], low_ref[...])
    side = jnp.exp((2.0 * gram - row_sq_ref[...] - head_sq_ref[...]) * (gamma_scale / D))
    solved = lax.dot_general(
        side, inverse_ref[...], (((1,), (1,)), ((), ())),
        precision=lax.Precision.HIGHEST, preferred_element_type=jnp.float32,
    )
    row = lax.broadcasted_iota(jnp.int32, side.shape, 0) + (start_ref[0] + step * TALL)
    panel_ref[...] = jnp.where(row < PANEL, lower_ref[...], solved)
    weight_ref[...] = full(jnp.where(row < PANEL, 0.0, solved), inverse_ref[...])


def panel_rows(starts, row_high, row_low, head, row_sq, head_sq, inverse, lower):
    height, depth = row_high.shape
    whole = lambda i, s: (0, 0)
    rows = lambda i, s: (i, 0)
    last = PANEL // TALL - 1
    out = jax.ShapeDtypeStruct((height, PANEL), jnp.float32)
    return pl.pallas_call(
        panel_kernel,
        out_shape=(out, out),
        grid_spec=pltpu.PrefetchScalarGridSpec(
            num_scalar_prefetch=1,
            grid=(height // TALL,),
            in_specs=[
                pl.BlockSpec((TALL, depth), rows),
                pl.BlockSpec((TALL, depth), rows),
                pl.BlockSpec((depth, PANEL), whole),
                pl.BlockSpec((TALL, 1), rows),
                pl.BlockSpec((1, PANEL), whole),
                pl.BlockSpec((PANEL, PANEL), whole),
                pl.BlockSpec((TALL, PANEL), lambda i, s: (jnp.minimum(i, last), 0)),
            ],
            out_specs=(pl.BlockSpec((TALL, PANEL), rows), pl.BlockSpec((TALL, PANEL), rows)),
            scratch_shapes=[pltpu.VMEM((depth, PANEL), jnp.bfloat16)] * 2,
        ),
        name="panel_rows",
    )(starts, row_high, row_low, head, row_sq[:, None], head_sq[None, :], inverse, lower)


def tile_kernel(
    start_ref, row_high_ref, row_low_ref, col_ref, row_sq_ref, col_sq_ref, weight_ref, far_ref, out_ref, high_ref, low_ref
):
    step = pl.program_id(0)

    @pl.when(step == 0)
    def _():
        split_into(col_ref[...], high_ref, low_ref)

    gram = gram_of(row_high_ref[...], row_low_ref[...], high_ref[...], low_ref[...])
    tile = jnp.exp((2.0 * gram - row_sq_ref[...] - col_sq_ref[...]) * (gamma_scale / D))
    row = lax.broadcasted_iota(jnp.int32, tile.shape, 0) + (start_ref[0] + step * TALL)
    col = lax.broadcasted_iota(jnp.int32, tile.shape, 1) + start_ref[1]
    tile = tile + jnp.where(row == col, ridge_value, 0.0)
    out_ref[...] = tile - full(weight_ref[...], far_ref[...])


def trailing_tile(starts, row_high, row_low, col_feat, row_sq, col_sq, weight, far):
    height, depth = row_high.shape
    width = col_feat.shape[1]
    return pl.pallas_call(
        tile_kernel,
        out_shape=jax.ShapeDtypeStruct((height, width), jnp.float32),
        grid_spec=pltpu.PrefetchScalarGridSpec(
            num_scalar_prefetch=1,
            grid=(height // TALL,),
            in_specs=[
                pl.BlockSpec((TALL, depth), lambda i, s: (i, 0)),
                pl.BlockSpec((TALL, depth), lambda i, s: (i, 0)),
                pl.BlockSpec((depth, width), lambda i, s: (0, 0)),
                pl.BlockSpec((TALL, 1), lambda i, s: (i, 0)),
                pl.BlockSpec((1, width), lambda i, s: (0, 0)),
                pl.BlockSpec((TALL, PANEL), lambda i, s: (i, 0)),
                pl.BlockSpec((PANEL, width), lambda i, s: (0, 0)),
            ],
            out_specs=pl.BlockSpec((TALL, width), lambda i, s: (i, 0)),
            scratch_shapes=[pltpu.VMEM((depth, width), jnp.bfloat16)] * 2,
        ),
        name="trailing_tile",
    )(starts, row_high, row_low, col_feat, row_sq[:, None], col_sq[None, :], weight, far)


def gauss(left, right, left_sq, right_sq):
    distance = left_sq[:, None] + right_sq[None, :] - 2.0 * product(left, right, 0, 0, lax.Precision.HIGH)
    return jnp.exp(-distance * (gamma_scale / D))


def squares(value):
    return jnp.sum(value * value, axis=0)


def ring(value, axis, size):
    at = lax.axis_index(axis)
    up = [(i, (i + 1) % size) for i in range(size)]
    down = [(target, source) for source, target in up]
    got = [(at, value)]
    above = below = value
    for step in range(1, size // 2 + 1):
        below = lax.ppermute(below, axis, up)
        got.append(((at - step) & (size - 1), below))
        if 2 * step < size:
            above = lax.ppermute(above, axis, down)
            got.append(((at + step) & (size - 1), above))
    return got


def swap(value):
    return lax.ppermute(value, "core", [(0, 1), (1, 0)])


def head_share(slices):
    y, core = lax.axis_index("y"), lax.axis_index("core")
    half = PANEL // CORES
    other = lax.ppermute(slices[:, half:PANEL], "core", [(0, 1)])
    own = jnp.where(core == 0, slices[:, :half], other)
    span = YS // 2
    while span:
        moved = lax.ppermute(own, "y", [(i, i + span) for i in range(0, YS, 2 * span)])
        own = jnp.where(y & (2 * span - 1) == span, moved, own)
        span //= 2
    return own


def head_of(own):
    core = lax.axis_index("core")
    depth, half = own.shape
    line = lax.all_gather(own, "x")
    plane = jnp.zeros((XS, ZS, depth, half), jnp.float32)
    for member, piece in ring(line, "z", ZS):
        plane = lax.dynamic_update_slice(plane, piece[:, None], (0, member, 0, 0))
    mine = plane.reshape(XS * ZS * depth, half)
    theirs = swap(mine)
    first = jnp.where(core == 0, mine, theirs)
    second = jnp.where(core == 0, theirs, mine)
    return jnp.concatenate([first, second], axis=1)


def column_share(slices):
    x, z = lax.axis_index("x"), lax.axis_index("z")
    rows, cols = YS * CORES, XS * ZS
    col = x * ZS + z
    odd = col & 1
    same, cross = [], []
    for r in range(rows):
        for c in range(cols):
            target = (c // 2 + r) % rows
            same.append((r * cols + c, target * cols + 2 * r + c % 2))
            cross.append((r * cols + c, target * cols + 2 * r + 1 - c % 2))
    left, right = slices[:, :PANEL], slices[:, PANEL:]
    like = lax.ppermute(jnp.where(odd == 0, left, right), ROW + COL, same)
    unlike = lax.ppermute(jnp.where(odd == 0, right, left), ROW + COL, cross)
    return jnp.concatenate([jnp.where(odd == 0, like, unlike), jnp.where(odd == 0, unlike, like)], axis=0)


def columns_of(shares):
    turn = (lax.axis_index("x") * ZS + lax.axis_index("z")) >> 1
    shares = lax.dynamic_slice_in_dim(jnp.concatenate([shares, shares], axis=0), turn, YS * CORES, 0)
    return shares.reshape(-1, PANEL)


def on_device(features):
    slices = features.T
    height = features.shape[0]
    row_id = lax.axis_index("y") * CORES + lax.axis_index("core")
    col_id = lax.axis_index("x") * ZS + lax.axis_index("z")
    piece = column_share(slices)
    slices, piece = lax.optimization_barrier((slices, piece))
    row_feat = lax.all_gather(slices, COL, axis=0, tiled=True)
    head = head_of(head_share(slices))
    piece, head = lax.optimization_barrier((piece, head))
    shares = lax.all_gather(piece, ROW)
    head_sq = squares(head)
    eye = jnp.eye(PANEL, dtype=jnp.float32)
    corner = gauss(head, head, head_sq, head_sq) + ridge_value * eye
    lower, inverse = factor(corner)
    row_sq = squares(row_feat)
    row_turned = row_feat.T
    row_high = lax.reduce_precision(row_turned, 8, 7)
    row_low = (row_turned - row_high).astype(jnp.bfloat16)
    row_high = row_high.astype(jnp.bfloat16)
    starts = jnp.stack([row_id * height, col_id * PANEL]).astype(jnp.int32)
    panel, weight = panel_rows(starts, row_high, row_low, head, row_sq, head_sq, inverse, lower)
    shares, weight = lax.optimization_barrier((shares, weight))
    col_feat = columns_of(shares)
    col_sq = squares(col_feat)
    far = jnp.where(col_id == 0, 0.0, gauss(head, col_feat, head_sq, col_sq))
    trailing = trailing_tile(starts, row_high, row_low, col_feat, row_sq, col_sq, weight, far)
    return (panel, trailing)


def solution(mesh):
    fine = Mesh(mesh.devices.reshape(YS, CORES, XS, ZS), ROW + COL)
    return jax.shard_map(
        on_device,
        mesh=fine,
        in_specs=(P(ROW, COL),),
        out_specs=(P(ROW, None), P(ROW, COL)),
        check_vma=False,
    )
```

```python
import jax
import jax.numpy as jnp
from jax import lax
from jax.experimental import pallas as pl
from jax.experimental.pallas import tpu as pltpu
from jax.sharding import Mesh
from jax.sharding import PartitionSpec as P

D = 1536
PANEL = 512
BLOCK = 128
GROUP = 4
TALL = 256
ROW = ("y", "core")
COL = ("x", "z")
YS, CORES, XS, ZS = 8, 2, 4, 8


gamma_scale = 0.6
ridge_value = 0.05


def full(a, b):
    return jnp.dot(a, b, precision=lax.Precision.HIGHEST, preferred_element_type=jnp.float32)


def product(a, b, on_a, on_b, precision=lax.Precision.HIGHEST):
    return lax.dot_general(
        a, b, (((on_a,), (on_b,)), ((), ())), precision=precision, preferred_element_type=jnp.float32
    )


def factor_block(rows):
    sub = lax.broadcasted_iota(jnp.int32, (8, BLOCK), 0)
    lane = lax.broadcasted_iota(jnp.int32, (8, BLOCK), 1)
    count = BLOCK // 8
    rows = list(rows)
    unit = [jnp.where(lane == sub + 8 * v, 1.0, 0.0).astype(jnp.float32) for v in range(count)]
    scale = [jnp.zeros((8, BLOCK), jnp.float32) for _ in range(count)]

    def column(v, j):
        return jnp.broadcast_to(rows[v][:, j : j + 1], (8, BLOCK))

    for start in range(0, BLOCK, GROUP):
        v0, o = start // 8, start % 8
        head = [column(v0, start + k) for k in range(GROUP)]
        inv, coef = [], {}
        for k in range(GROUP):
            pivot = head[k][o + k : o + k + 1, :]
            inv.append(1.0 / pivot)
            root = lax.rsqrt(pivot)
            scale[v0] = jnp.where(sub == o + k, root, scale[v0])
            for l in range(k + 1, GROUP):
                coef[k, l] = inv[k] * head[k][o + l : o + l + 1, :]
                head[l] = head[l] - head[k] * coef[k, l]
        top = [rows[v0][o + k : o + k + 1, :] for k in range(GROUP)]
        top_unit = [unit[v0][o + k : o + k + 1, :] for k in range(GROUP)]
        for k in range(GROUP):
            for l in range(k + 1, GROUP):
                top[l] = top[l] - coef[k, l] * top[k]
                top_unit[l] = top_unit[l] - coef[k, l] * top_unit[k]
        for v in range(v0, count):
            if v == v0:
                part = head
            else:
                part = [column(v, start + k) for k in range(GROUP)]
                for k in range(GROUP):
                    for l in range(k + 1, GROUP):
                        part[l] = part[l] - part[k] * coef[k, l]
            new_row, new_unit = rows[v], unit[v]
            for k in range(GROUP):
                factor = part[k] * inv[k]
                if v == v0:
                    factor = jnp.where(sub > o + k, factor, 0.0)
                new_row = new_row - factor * top[k]
                new_unit = new_unit - factor * top_unit[k]
            rows[v], unit[v] = new_row, new_unit
    rows = [jnp.where(lane >= sub + 8 * v, rows[v] * scale[v], 0.0) for v in range(count)]
    unit = [unit[v] * scale[v] for v in range(count)]
    return jnp.concatenate(rows, axis=0), jnp.concatenate(unit, axis=0)


def factor_kernel(corner_ref, lower_ref, inverse_ref, work_ref):
    work_ref[...] = corner_ref[...]
    inverse_ref[...] = jnp.zeros((PANEL, PANEL), jnp.float32)

    def update(at, upper, inv):
        end = at + BLOCK
        lower_ref[at:end, at:end] = upper.T
        if at:
            inverse_ref[at:end, :at] = full(inv, inverse_ref[at:end, :at])
        inverse_ref[at:end, at:end] = inv
        if end < PANEL:
            lower_ref[at:end, end:] = jnp.zeros((BLOCK, PANEL - end), jnp.float32)
            right = full(inv, work_ref[at:end, end:])
            below = right.T
            lower_ref[end:, at:end] = below
            work_ref[end:, end:] -= full(below, right)
            inverse_ref[end:, :end] -= full(below, inverse_ref[at:end, :end])

    @pl.loop(0, PANEL // BLOCK)
    def _(index):
        at = pl.multiple_of(index * BLOCK, BLOCK)
        block = work_ref[pl.ds(at, BLOCK), pl.ds(at, BLOCK)]
        upper, inv = factor_block([block[8 * v : 8 * v + 8] for v in range(BLOCK // 8)])
        for which in range(PANEL // BLOCK):

            @pl.when(index == which)
            def _():
                update(which * BLOCK, upper, inv)


def factor(corner):
    square = jax.ShapeDtypeStruct((PANEL, PANEL), jnp.float32)
    return pl.pallas_call(
        factor_kernel, out_shape=(square, square),
        scratch_shapes=[pltpu.VMEM((PANEL, PANEL), jnp.float32)], name="factor",
    )(corner)


def split(value):
    high = value.astype(jnp.bfloat16)
    return high, (value - high.astype(jnp.float32)).astype(jnp.bfloat16)


def gram_of(rows, high, low):
    def inner(a, b):
        return lax.dot_general(a, b, (((0,), (0,)), ((), ())), preferred_element_type=jnp.float32)

    row_high, row_low = split(rows)
    return inner(row_high, high) + (inner(row_high, low) + inner(row_low, high))


def panel_kernel(
    start_ref, row_ref, head_ref, head_sq_ref, inverse_ref, lower_ref,
    panel_ref, weight_ref, row_sq_ref, high_ref, low_ref,
):
    step = pl.program_id(0)

    @pl.when(step == 0)
    def _():
        high_ref[...], low_ref[...] = split(head_ref[...])

    rows = row_ref[...]
    row_sq = jnp.broadcast_to(jnp.sum(rows * rows, axis=0, keepdims=True), (8, TALL)).T[:, :1]
    row_sq_ref[...] = row_sq
    gram = gram_of(rows, high_ref[...], low_ref[...])
    side = jnp.exp((2.0 * gram - row_sq - head_sq_ref[...]) * (gamma_scale / D))
    solved = lax.dot_general(
        side, inverse_ref[...], (((1,), (1,)), ((), ())),
        precision=lax.Precision.HIGHEST, preferred_element_type=jnp.float32,
    )
    row = lax.broadcasted_iota(jnp.int32, side.shape, 0) + (start_ref[0] + step * TALL)
    panel_ref[...] = jnp.where(row < PANEL, lower_ref[...], solved)
    weight_ref[...] = full(jnp.where(row < PANEL, 0.0, solved), inverse_ref[...])


def panel_rows(starts, row_feat, head, head_sq, inverse, lower):
    depth, height = row_feat.shape
    whole = lambda i, s: (0, 0)
    rows = lambda i, s: (i, 0)
    last = PANEL // TALL - 1
    out = jax.ShapeDtypeStruct((height, PANEL), jnp.float32)
    return pl.pallas_call(
        panel_kernel,
        out_shape=(out, out, jax.ShapeDtypeStruct((height, 1), jnp.float32)),
        grid_spec=pltpu.PrefetchScalarGridSpec(
            num_scalar_prefetch=1,
            grid=(height // TALL,),
            in_specs=[
                pl.BlockSpec((depth, TALL), lambda i, s: (0, i)),
                pl.BlockSpec((depth, PANEL), whole),
                pl.BlockSpec((1, PANEL), whole),
                pl.BlockSpec((PANEL, PANEL), whole),
                pl.BlockSpec((TALL, PANEL), lambda i, s: (jnp.minimum(i, last), 0)),
            ],
            out_specs=(pl.BlockSpec((TALL, PANEL), rows), pl.BlockSpec((TALL, PANEL), rows), pl.BlockSpec((TALL, 1), rows)),
            scratch_shapes=[pltpu.VMEM((depth, PANEL), jnp.bfloat16)] * 2,
        ),
        name="panel_rows",
    )(starts, row_feat, head, head_sq[None, :], inverse, lower)


def tile_kernel(start_ref, row_ref, col_ref, row_sq_ref, col_sq_ref, weight_ref, far_ref, out_ref, high_ref, low_ref):
    step = pl.program_id(0)

    @pl.when(step == 0)
    def _():
        high_ref[...], low_ref[...] = split(col_ref[...])

    gram = gram_of(row_ref[...], high_ref[...], low_ref[...])
    tile = jnp.exp((2.0 * gram - row_sq_ref[...] - col_sq_ref[...]) * (gamma_scale / D))
    row = lax.broadcasted_iota(jnp.int32, tile.shape, 0) + (start_ref[0] + step * TALL)
    col = lax.broadcasted_iota(jnp.int32, tile.shape, 1) + start_ref[1]
    tile = tile + jnp.where(row == col, ridge_value, 0.0)
    out_ref[...] = tile - full(weight_ref[...], far_ref[...])


def trailing_tile(starts, row_feat, col_feat, row_sq, col_sq, weight, far):
    depth, height = row_feat.shape
    width = col_feat.shape[1]
    return pl.pallas_call(
        tile_kernel,
        out_shape=jax.ShapeDtypeStruct((height, width), jnp.float32),
        grid_spec=pltpu.PrefetchScalarGridSpec(
            num_scalar_prefetch=1,
            grid=(height // TALL,),
            in_specs=[
                pl.BlockSpec((depth, TALL), lambda i, s: (0, i)),
                pl.BlockSpec((depth, width), lambda i, s: (0, 0)),
                pl.BlockSpec((TALL, 1), lambda i, s: (i, 0)),
                pl.BlockSpec((1, width), lambda i, s: (0, 0)),
                pl.BlockSpec((TALL, PANEL), lambda i, s: (i, 0)),
                pl.BlockSpec((PANEL, width), lambda i, s: (0, 0)),
            ],
            out_specs=pl.BlockSpec((TALL, width), lambda i, s: (i, 0)),
            scratch_shapes=[pltpu.VMEM((depth, width), jnp.bfloat16)] * 2,
        ),
        name="trailing_tile",
    )(starts, row_feat, col_feat, row_sq, col_sq[None, :], weight, far)


def gauss(left, right, left_sq, right_sq):
    distance = left_sq[:, None] + right_sq[None, :] - 2.0 * product(left, right, 0, 0, lax.Precision.HIGH)
    return jnp.exp(-distance * (gamma_scale / D))


def squares(value):
    return jnp.sum(value * value, axis=0)


def ring(value, axis, size):
    at = lax.axis_index(axis)
    up = [(i, (i + 1) % size) for i in range(size)]
    down = [(target, source) for source, target in up]
    got = [(at, value)]
    above = below = value
    for step in range(1, size // 2 + 1):
        below = lax.ppermute(below, axis, up)
        got.append(((at - step) & (size - 1), below))
        if 2 * step < size:
            above = lax.ppermute(above, axis, down)
            got.append(((at + step) & (size - 1), above))
    return got


def swap(value):
    return lax.ppermute(value, "core", [(0, 1), (1, 0)])


def head_share(slices):
    y, core = lax.axis_index("y"), lax.axis_index("core")
    half = PANEL // CORES
    other = lax.ppermute(slices[:, half:PANEL], "core", [(0, 1)])
    own = jnp.where(core == 0, slices[:, :half], other)
    span = YS // 2
    while span:
        moved = lax.ppermute(own, "y", [(i, i + span) for i in range(0, YS, 2 * span)])
        own = jnp.where(y & (2 * span - 1) == span, moved, own)
        span //= 2
    return own


def head_of(own):
    core = lax.axis_index("core")
    depth, half = own.shape
    line = lax.all_gather(own, "x")
    plane = jnp.zeros((XS, ZS, depth, half), jnp.float32)
    for member, piece in ring(line, "z", ZS):
        plane = lax.dynamic_update_slice(plane, piece[:, None], (0, member, 0, 0))
    mine = plane.reshape(XS * ZS * depth, half)
    theirs = swap(mine)
    first = jnp.where(core == 0, mine, theirs)
    second = jnp.where(core == 0, theirs, mine)
    return jnp.concatenate([first, second], axis=1)


def column_share(slices):
    x, z = lax.axis_index("x"), lax.axis_index("z")
    rows, cols = YS * CORES, XS * ZS
    col = x * ZS + z
    odd = col & 1
    same, cross = [], []
    for r in range(rows):
        for c in range(cols):
            target = (c // 2 + r) % rows
            same.append((r * cols + c, target * cols + 2 * r + c % 2))
            cross.append((r * cols + c, target * cols + 2 * r + 1 - c % 2))
    left, right = slices[:, :PANEL], slices[:, PANEL:]
    like = lax.ppermute(jnp.where(odd == 0, left, right), ROW + COL, same)
    unlike = lax.ppermute(jnp.where(odd == 0, right, left), ROW + COL, cross)
    return jnp.concatenate([jnp.where(odd == 0, like, unlike), jnp.where(odd == 0, unlike, like)], axis=0)


def columns_of(shares):
    turn = (lax.axis_index("x") * ZS + lax.axis_index("z")) >> 1
    shares = lax.dynamic_slice_in_dim(jnp.concatenate([shares, shares], axis=0), turn, YS * CORES, 0)
    return shares.reshape(-1, PANEL)


def on_device(features):
    slices = features.T
    height = features.shape[0]
    row_id = lax.axis_index("y") * CORES + lax.axis_index("core")
    col_id = lax.axis_index("x") * ZS + lax.axis_index("z")
    piece = column_share(slices)
    slices, piece = lax.optimization_barrier((slices, piece))
    row_feat = lax.all_gather(slices, COL, axis=0, tiled=True)
    head = head_of(head_share(slices))
    piece, head = lax.optimization_barrier((piece, head))
    shares = lax.all_gather(piece, ROW)
    head_sq = squares(head)
    eye = jnp.eye(PANEL, dtype=jnp.float32)
    corner = gauss(head, head, head_sq, head_sq) + ridge_value * eye
    lower, inverse = factor(corner)
    starts = jnp.stack([row_id * height, col_id * PANEL]).astype(jnp.int32)
    panel, weight, row_sq = panel_rows(starts, row_feat, head, head_sq, inverse, lower)
    shares, weight = lax.optimization_barrier((shares, weight))
    col_feat = columns_of(shares)
    col_sq = squares(col_feat)
    far = jnp.where(col_id == 0, 0.0, gauss(head, col_feat, head_sq, col_sq))
    trailing = trailing_tile(starts, row_feat, col_feat, row_sq, col_sq, weight, far)
    return (panel, trailing)


def solution(mesh):
    fine = Mesh(mesh.devices.reshape(YS, CORES, XS, ZS), ROW + COL)
    return jax.shard_map(
        on_device,
        mesh=fine,
        in_specs=(P(ROW, COL),),
        out_specs=(P(ROW, None), P(ROW, COL)),
        check_vma=False,
    )
```

```python
import jax
import jax.numpy as jnp
from jax import lax
from jax.experimental import pallas as pl
from jax.experimental.pallas import tpu as pltpu
from jax.sharding import Mesh
from jax.sharding import PartitionSpec as P

D = 1536
PANEL = 512
BLOCK = 128
GROUP = 8
TALL = 256
ROW = ("y", "core")
COL = ("x", "z")
YS, CORES, XS, ZS = 8, 2, 4, 8


gamma_scale = 0.6
ridge_value = 0.05


def full(a, b):
    return jnp.dot(a, b, precision=lax.Precision.HIGHEST, preferred_element_type=jnp.float32)


def product(a, b, on_a, on_b, precision=lax.Precision.HIGHEST):
    return lax.dot_general(
        a, b, (((on_a,), (on_b,)), ((), ())), precision=precision, preferred_element_type=jnp.float32
    )


def factor_block(rows):
    sub = lax.broadcasted_iota(jnp.int32, (8, BLOCK), 0)
    lane = lax.broadcasted_iota(jnp.int32, (8, BLOCK), 1)
    count = BLOCK // 8
    rows = list(rows)
    unit = [jnp.where(lane == sub + 8 * v, 1.0, 0.0).astype(jnp.float32) for v in range(count)]
    scale = [jnp.zeros((8, BLOCK), jnp.float32) for _ in range(count)]

    def column(v, j):
        return jnp.broadcast_to(rows[v][:, j : j + 1], (8, BLOCK))

    for start in range(0, BLOCK, GROUP):
        v0, o = start // 8, start % 8
        head = [column(v0, start + k) for k in range(GROUP)]
        inv, coef = [], {}
        for k in range(GROUP):
            pivot = head[k][o + k : o + k + 1, :]
            inv.append(1.0 / pivot)
            root = lax.rsqrt(pivot)
            scale[v0] = jnp.where(sub == o + k, root, scale[v0])
            for l in range(k + 1, GROUP):
                coef[k, l] = inv[k] * head[k][o + l : o + l + 1, :]
                head[l] = head[l] - head[k] * coef[k, l]
        top = [rows[v0][o + k : o + k + 1, :] for k in range(GROUP)]
        top_unit = [unit[v0][o + k : o + k + 1, :] for k in range(GROUP)]
        for k in range(GROUP):
            for l in range(k + 1, GROUP):
                top[l] = top[l] - coef[k, l] * top[k]
                top_unit[l] = top_unit[l] - coef[k, l] * top_unit[k]
        for v in range(v0, count):
            if v == v0:
                part = head
            else:
                part = [column(v, start + k) for k in range(GROUP)]
                for k in range(GROUP):
                    for l in range(k + 1, GROUP):
                        part[l] = part[l] - part[k] * coef[k, l]
            new_row, new_unit = rows[v], unit[v]
            for k in range(GROUP):
                factor = part[k] * inv[k]
                if v == v0:
                    factor = jnp.where(sub > o + k, factor, 0.0)
                new_row = new_row - factor * top[k]
                new_unit = new_unit - factor * top_unit[k]
            rows[v], unit[v] = new_row, new_unit
    rows = [jnp.where(lane >= sub + 8 * v, rows[v] * scale[v], 0.0) for v in range(count)]
    unit = [unit[v] * scale[v] for v in range(count)]
    return jnp.concatenate(rows, axis=0), jnp.concatenate(unit, axis=0)


def factor_kernel(corner_ref, lower_ref, inverse_ref, work_ref):
    work_ref[...] = corner_ref[...]
    inverse_ref[...] = jnp.zeros((PANEL, PANEL), jnp.float32)

    def update(at, upper, inv):
        end = at + BLOCK
        lower_ref[at:end, at:end] = upper.T
        if at:
            inverse_ref[at:end, :at] = full(inv, inverse_ref[at:end, :at])
        inverse_ref[at:end, at:end] = inv
        if end < PANEL:
            lower_ref[at:end, end:] = jnp.zeros((BLOCK, PANEL - end), jnp.float32)
            right = full(inv, work_ref[at:end, end:])
            below = right.T
            lower_ref[end:, at:end] = below
            work_ref[end:, end:] -= full(below, right)
            inverse_ref[end:, :end] -= full(below, inverse_ref[at:end, :end])

    @pl.loop(0, PANEL // BLOCK)
    def _(index):
        at = pl.multiple_of(index * BLOCK, BLOCK)
        block = work_ref[pl.ds(at, BLOCK), pl.ds(at, BLOCK)]
        upper, inv = factor_block([block[8 * v : 8 * v + 8] for v in range(BLOCK // 8)])
        for which in range(PANEL // BLOCK):

            @pl.when(index == which)
            def _():
                update(which * BLOCK, upper, inv)


def factor(corner):
    square = jax.ShapeDtypeStruct((PANEL, PANEL), jnp.float32)
    return pl.pallas_call(
        factor_kernel, out_shape=(square, square),
        scratch_shapes=[pltpu.VMEM((PANEL, PANEL), jnp.float32)], name="factor",
    )(corner)


def split(value):
    high = value.astype(jnp.bfloat16)
    return high, (value - high.astype(jnp.float32)).astype(jnp.bfloat16)


def gram_of(rows, high, low):
    def inner(a, b):
        return lax.dot_general(a, b, (((0,), (0,)), ((), ())), preferred_element_type=jnp.float32)

    row_high, row_low = split(rows)
    return inner(row_high, high) + (inner(row_high, low) + inner(row_low, high))


def panel_kernel(
    start_ref, row_ref, head_ref, head_sq_ref, inverse_ref, lower_ref,
    panel_ref, weight_ref, row_sq_ref, high_ref, low_ref,
):
    step = pl.program_id(0)

    @pl.when(step == 0)
    def _():
        high_ref[...], low_ref[...] = split(head_ref[...])

    rows = row_ref[...]
    row_sq = jnp.broadcast_to(jnp.sum(rows * rows, axis=0, keepdims=True), (8, TALL)).T[:, :1]
    row_sq_ref[...] = row_sq
    gram = gram_of(rows, high_ref[...], low_ref[...])
    side = jnp.exp((2.0 * gram - row_sq - head_sq_ref[...]) * (gamma_scale / D))
    solved = lax.dot_general(
        side, inverse_ref[...], (((1,), (1,)), ((), ())),
        precision=lax.Precision.HIGHEST, preferred_element_type=jnp.float32,
    )
    row = lax.broadcasted_iota(jnp.int32, side.shape, 0) + (start_ref[0] + step * TALL)
    panel_ref[...] = jnp.where(row < PANEL, lower_ref[...], solved)
    weight_ref[...] = full(jnp.where(row < PANEL, 0.0, solved), inverse_ref[...])


def panel_rows(starts, row_feat, head, head_sq, inverse, lower):
    depth, height = row_feat.shape
    whole = lambda i, s: (0, 0)
    rows = lambda i, s: (i, 0)
    last = PANEL // TALL - 1
    out = jax.ShapeDtypeStruct((height, PANEL), jnp.float32)
    return pl.pallas_call(
        panel_kernel,
        out_shape=(out, out, jax.ShapeDtypeStruct((height, 1), jnp.float32)),
        grid_spec=pltpu.PrefetchScalarGridSpec(
            num_scalar_prefetch=1,
            grid=(height // TALL,),
            in_specs=[
                pl.BlockSpec((depth, TALL), lambda i, s: (0, i)),
                pl.BlockSpec((depth, PANEL), whole),
                pl.BlockSpec((1, PANEL), whole),
                pl.BlockSpec((PANEL, PANEL), whole),
                pl.BlockSpec((TALL, PANEL), lambda i, s: (jnp.minimum(i, last), 0)),
            ],
            out_specs=(pl.BlockSpec((TALL, PANEL), rows), pl.BlockSpec((TALL, PANEL), rows), pl.BlockSpec((TALL, 1), rows)),
            scratch_shapes=[pltpu.VMEM((depth, PANEL), jnp.bfloat16)] * 2,
        ),
        name="panel_rows",
    )(starts, row_feat, head, head_sq[None, :], inverse, lower)


def tile_kernel(start_ref, row_ref, col_ref, row_sq_ref, col_sq_ref, weight_ref, far_ref, out_ref, high_ref, low_ref):
    step = pl.program_id(0)

    @pl.when(step == 0)
    def _():
        high_ref[...], low_ref[...] = split(col_ref[...])

    gram = gram_of(row_ref[...], high_ref[...], low_ref[...])
    tile = jnp.exp((2.0 * gram - row_sq_ref[...] - col_sq_ref[...]) * (gamma_scale / D))
    row = lax.broadcasted_iota(jnp.int32, tile.shape, 0) + (start_ref[0] + step * TALL)
    col = lax.broadcasted_iota(jnp.int32, tile.shape, 1) + start_ref[1]
    tile = tile + jnp.where(row == col, ridge_value, 0.0)
    out_ref[...] = tile - full(weight_ref[...], far_ref[...])


def trailing_tile(starts, row_feat, col_feat, row_sq, col_sq, weight, far):
    depth, height = row_feat.shape
    width = col_feat.shape[1]
    return pl.pallas_call(
        tile_kernel,
        out_shape=jax.ShapeDtypeStruct((height, width), jnp.float32),
        grid_spec=pltpu.PrefetchScalarGridSpec(
            num_scalar_prefetch=1,
            grid=(height // TALL,),
            in_specs=[
                pl.BlockSpec((depth, TALL), lambda i, s: (0, i)),
                pl.BlockSpec((depth, width), lambda i, s: (0, 0)),
                pl.BlockSpec((TALL, 1), lambda i, s: (i, 0)),
                pl.BlockSpec((1, width), lambda i, s: (0, 0)),
                pl.BlockSpec((TALL, PANEL), lambda i, s: (i, 0)),
                pl.BlockSpec((PANEL, width), lambda i, s: (0, 0)),
            ],
            out_specs=pl.BlockSpec((TALL, width), lambda i, s: (i, 0)),
            scratch_shapes=[pltpu.VMEM((depth, width), jnp.bfloat16)] * 2,
        ),
        name="trailing_tile",
    )(starts, row_feat, col_feat, row_sq, col_sq[None, :], weight, far)


def gauss(left, right, left_sq, right_sq):
    distance = left_sq[:, None] + right_sq[None, :] - 2.0 * product(left, right, 0, 0, lax.Precision.HIGH)
    return jnp.exp(-distance * (gamma_scale / D))


def squares(value):
    return jnp.sum(value * value, axis=0)


def ring(value, axis, size):
    at = lax.axis_index(axis)
    up = [(i, (i + 1) % size) for i in range(size)]
    down = [(target, source) for source, target in up]
    got = [(at, value)]
    above = below = value
    for step in range(1, size // 2 + 1):
        below = lax.ppermute(below, axis, up)
        got.append(((at - step) & (size - 1), below))
        if 2 * step < size:
            above = lax.ppermute(above, axis, down)
            got.append(((at + step) & (size - 1), above))
    return got


def swap(value):
    return lax.ppermute(value, "core", [(0, 1), (1, 0)])


def head_share(slices):
    y, core = lax.axis_index("y"), lax.axis_index("core")
    half = PANEL // CORES
    other = lax.ppermute(slices[:, half:PANEL], "core", [(0, 1)])
    own = jnp.where(core == 0, slices[:, :half], other)
    span = YS // 2
    while span:
        moved = lax.ppermute(own, "y", [(i, i + span) for i in range(0, YS, 2 * span)])
        own = jnp.where(y & (2 * span - 1) == span, moved, own)
        span //= 2
    return own


def head_of(own):
    core = lax.axis_index("core")
    depth, half = own.shape
    line = lax.all_gather(own, "x")
    plane = jnp.zeros((XS, ZS, depth, half), jnp.float32)
    for member, piece in ring(line, "z", ZS):
        plane = lax.dynamic_update_slice(plane, piece[:, None], (0, member, 0, 0))
    mine = plane.reshape(XS * ZS * depth, half)
    theirs = swap(mine)
    first = jnp.where(core == 0, mine, theirs)
    second = jnp.where(core == 0, theirs, mine)
    return jnp.concatenate([first, second], axis=1)


def column_share(slices):
    x, z = lax.axis_index("x"), lax.axis_index("z")
    rows, cols = YS * CORES, XS * ZS
    col = x * ZS + z
    odd = col & 1
    same, cross = [], []
    for r in range(rows):
        for c in range(cols):
            target = (c // 2 + r) % rows
            same.append((r * cols + c, target * cols + 2 * r + c % 2))
            cross.append((r * cols + c, target * cols + 2 * r + 1 - c % 2))
    left, right = slices[:, :PANEL], slices[:, PANEL:]
    like = lax.ppermute(jnp.where(odd == 0, left, right), ROW + COL, same)
    unlike = lax.ppermute(jnp.where(odd == 0, right, left), ROW + COL, cross)
    return jnp.concatenate([jnp.where(odd == 0, like, unlike), jnp.where(odd == 0, unlike, like)], axis=0)


def columns_of(shares):
    turn = (lax.axis_index("x") * ZS + lax.axis_index("z")) >> 1
    shares = lax.dynamic_slice_in_dim(jnp.concatenate([shares, shares], axis=0), turn, YS * CORES, 0)
    return shares.reshape(-1, PANEL)


def on_device(features):
    slices = features.T
    height = features.shape[0]
    row_id = lax.axis_index("y") * CORES + lax.axis_index("core")
    col_id = lax.axis_index("x") * ZS + lax.axis_index("z")
    piece = column_share(slices)
    slices, piece = lax.optimization_barrier((slices, piece))
    row_feat = lax.all_gather(slices, COL, axis=0, tiled=True)
    head = head_of(head_share(slices))
    piece, head = lax.optimization_barrier((piece, head))
    shares = lax.all_gather(piece, ROW)
    head_sq = squares(head)
    eye = jnp.eye(PANEL, dtype=jnp.float32)
    corner = gauss(head, head, head_sq, head_sq) + ridge_value * eye
    lower, inverse = factor(corner)
    starts = jnp.stack([row_id * height, col_id * PANEL]).astype(jnp.int32)
    panel, weight, row_sq = panel_rows(starts, row_feat, head, head_sq, inverse, lower)
    shares, weight = lax.optimization_barrier((shares, weight))
    col_feat = columns_of(shares)
    col_sq = squares(col_feat)
    far = jnp.where(col_id == 0, 0.0, gauss(head, col_feat, head_sq, col_sq))
    trailing = trailing_tile(starts, row_feat, col_feat, row_sq, col_sq, weight, far)
    return (panel, trailing)


def solution(mesh):
    fine = Mesh(mesh.devices.reshape(YS, CORES, XS, ZS), ROW + COL)
    return jax.shard_map(
        on_device,
        mesh=fine,
        in_specs=(P(ROW, COL),),
        out_specs=(P(ROW, None), P(ROW, COL)),
        check_vma=False,
    )
```
